32 devices in a mesh: groups: 2 (over x), tok: 16 (over z, y, core).
Axes of the slice: x: 2, y: 2, z: 4, core: 2. Of those that a mesh axis runs over, the one named last changes fastest.
Arguments:
- queries: bfloat16 [4096, 4096], P(('groups', 'tok')), parts along dimension 0, may hold values from -8 to 8
- new_keys: bfloat16 [4096, 512], P(('groups', 'tok')), parts along dimension 0, may hold values from -8 to 8
- new_values: bfloat16 [4096, 512], P(('groups', 'tok')), parts along dimension 0, may hold values from -6 to 6
- cache_keys: bfloat16 [65536, 512], P(('groups', 'tok')), parts along dimension 0, may hold values from -8 to 8
- cache_values: bfloat16 [65536, 512], P(('groups', 'tok')), parts along dimension 0, may hold values from -6 to 6
- cache_lens: int32 [32], P(('groups', 'tok')), parts along dimension 0, may hold values from 1 to 2048, 20480 in all
- residual: bfloat16 [4096, 2048], P(('groups', 'tok')), parts along dimension 0, may hold values from -40 to 40
- out_weight: bfloat16 [4096, 2048], P('tok'), may hold values from -0.09375 to 0.09375
- norm_gain: float32 [2048], replicated, may hold values from 0.25 to 1.75
- expert_ids: int32 [4096, 8], P(('groups', 'tok')), parts along dimension 0, may hold values from 0 to 63, all different within a row; in each aligned block of 64 rows (0 to 63, 64 to 127, ...) at most 12 rows name the same one
- route_weights: float32 [4096, 8], P(('groups', 'tok')), parts along dimension 0, may hold values from 0.2 to 1
- gate_weight: bfloat16 [64, 2048, 384], P('tok'), may hold values from -0.125 to 0.125
- up_weight: bfloat16 [64, 2048, 384], P('tok'), may hold values from -0.125 to 0.125
- down_weight: bfloat16 [64, 384, 2048], P('tok'), may hold values from -0.3125 to 0.3125
Outputs:
- layer_out: bfloat16 [4096, 2048], P(('groups', 'tok')), parts along dimension 0
The draws below stay inside these ranges and needn't reach their ends.
There are 2 independent parts, one for each index of `groups`. The reference program is written for one: setup_inputs(seed, part) draws one part's arguments, and reference() takes and returns one part's arrays. A program takes and returns all parts, laid end to end along the dimension named above; an argument that names none is the same for every part. Nothing has to cross between parts.
Inputs may be any that keep to these rules, and one draw needn't show every extreme that they name: `expert_ids`: each row names 8 different experts. In each aligned block of 64 rows no expert is named by more than 12 rows; that many is reached in some block. `cache_lens`: the largest length equals 2048.
All inputs are finite; a program needn't handle non-finite values. No bound on the sum of `cache_lens` on one device may be relied on, other than what follows from the above.
Results may differ from the reference program's by a relative error of at most 0.009.
Values may be sent and summed in bfloat16 or wider, within the bound.
No kernel may reach another device: no remote copies, remote signals or barrier semaphores. Data moves between devices by JAX's collectives and lax.ppermute only.
A program may use at most 128 MiB of HBM per device.

```python
import math
import jax
import jax.numpy as jnp
import numpy as np
from jax import lax

D = 2048
HEADS = 32
KVH = 4
HD = 128
FF = 384
TOPK = 8
ROWS = 128
CACHE = 2048
EXPERTS = 64
REQUESTS = 16
TOKENS = 2048
BLOCK = 64
CAP = 12


def draw_queries(key, part):
    first = jax.random.fold_in(key, 11)
    values = jnp.clip(jax.random.normal(first, (REQUESTS * ROWS, HEADS * HD), jnp.float32), -6.0, 6.0)
    return values.astype(jnp.bfloat16)


def draw_cache_keys(key, part):
    first = jax.random.fold_in(key, 23)
    values = jnp.clip(jax.random.normal(first, (REQUESTS * CACHE, KVH * HD), jnp.float32), -6.0, 6.0)
    return values.astype(jnp.bfloat16)


def draw_new_keys(key, part):
    first = jax.random.fold_in(key, 37)
    values = jnp.clip(jax.random.normal(first, (REQUESTS * ROWS, KVH * HD), jnp.float32), -6.0, 6.0)
    return values.astype(jnp.bfloat16)


def draw_residual(key, part):
    first = jax.random.fold_in(key, 53)
    values = jnp.clip(jax.random.normal(first, (REQUESTS * ROWS, D), jnp.float32), -6.0, 6.0)
    return values.astype(jnp.bfloat16)


def levels(rng, shape, shards, low, top_value):
    def one(axis_at, shards_of):
        steps = jax.random.uniform(jax.random.fold_in(jax.random.fold_in(rng, 6), axis_at), (shards_of,), jnp.float32, low / len(shards), top_value / len(shards))
        return jnp.repeat(jnp.exp(steps), shape[axis_at] // shards_of).reshape((-1,) + (1,) * (len(shape) - axis_at - 1))

    gain = one(*shards[0])
    for cut in shards[1:]:
        gain = gain * one(*cut)
    return gain


def length_profile(count, total, bound, skew):
    portions = [(1 << 20) // math.isqrt(grade ** skew) + 1 for grade in range(2, count + 1)]
    surplus, holding = total - bound - (count - 1), [1] * (count - 1)
    while surplus > 0:
        candidates = [i for i in range(count - 1) if holding[i] < bound]
        mass, budget = sum([portions[i] for i in candidates]), surplus
        for i in candidates:
            addition = min(bound - holding[i], max(1, budget * portions[i] // mass), surplus)
            holding[i] = holding[i] + addition
            surplus = surplus - addition
    return np.array([bound] + holding)


def ragged_sizes(key, amount, total, most, lean):
    if amount == 2:
        one = jax.random.randint(key, (), max(1, total - most), min(most, total - 1) + 1)
        return jnp.stack([one, total - one])
    lengths = jnp.asarray(length_profile(amount, total, most, lean), jnp.int32)
    couples = (amount - 1) // 2
    source_of, receiver = lengths[1:1 + 2 * couples:2], lengths[2:2 + 2 * couples:2]
    slack = jnp.minimum(source_of - 1, most - receiver)
    moved = jax.random.randint(jax.random.fold_in(key, 1), (couples,), 0, 1 << 20) % (slack + 1)
    lengths = lengths.at[1:1 + 2 * couples:2].set(source_of - moved).at[2:2 + 2 * couples:2].set(receiver + moved)
    return lengths[jax.random.permutation(jax.random.fold_in(key, 2), amount)]


def assign_block(key, own, number, rows, number_of, top, most, skew):
    order = jax.random.permutation(key, number_of)
    packed, ordinary = load_shares(number_of, rows * top, most, skew, True), load_shares(number_of, rows * top, most, skew, False)
    places = jnp.arange(number_of)

    def named(tallies, offset_by):
        used = int((tallies > 0).sum())
        fixed = max(1, used // 4)
        moved = fixed + (places - fixed + offset_by * (used - fixed)) % max(1, number_of - fixed)
        return jnp.zeros((number_of,), jnp.int32).at[order[jnp.where(places < fixed, places, moved)]].set(jnp.asarray(tallies, jnp.int32))

    tallies = jnp.where(number % 4 == 0, named(packed, number // 4), named(ordinary, number - number // 4 - 1))
    mixed = jax.random.permutation(jax.random.fold_in(own, 3), number_of)
    giver, taker = mixed[0:number_of // 2 * 2:2], mixed[1:number_of // 2 * 2:2]
    margin = jnp.minimum(tallies[giver] - 1, most - tallies[taker]) // 2
    margin = jnp.where((giver == order[0]) | (taker == order[0]) | (tallies[taker] == 0), 0, jnp.maximum(margin, 0))
    moved = jax.random.randint(jax.random.fold_in(own, 4), (number_of // 2,), 0, 1 << 20) % (margin + 1)
    tallies = tallies.at[giver].add(-moved).at[taker].add(moved)
    items = jnp.searchsorted(jnp.cumsum(tallies), jnp.arange(rows * top), side="right").astype(jnp.int32)
    table = items.reshape(top, rows).T
    table = table[jax.random.permutation(jax.random.fold_in(own, 1), rows)]
    offset_by = jax.random.randint(jax.random.fold_in(own, 2), (rows, 1), 0, top)
    return jnp.take_along_axis(table, (jnp.arange(top)[None, :] + offset_by) % top, axis=1)


def load_shares(count, total, limit, lean, full):
    weights = [(1 << 20) // math.isqrt(rank ** lean) + 1 for rank in range(1, count + 1)]
    largest = limit if full else min(limit, max(-(-total // count), total * weights[0] // sum(weights)))
    least = 1 if total - largest >= count - 1 else 0
    holding, rest = [largest] + [least] * (count - 1), total - largest - least * (count - 1)
    while rest > 0:
        free = [i for i in range(1, count) if holding[i] < largest] or [i for i in range(1, count) if holding[i] < limit]
        pool, budget = sum([weights[i] for i in free]), rest
        for i in free:
            addition = min(limit - holding[i], max(1, budget * weights[i] // pool), rest)
            holding[i] = holding[i] + addition
            rest = rest - addition
    return np.array(holding)


def normal_values(rng, extent, deviation, most, split=(), held_as=jnp.bfloat16):
    entries = deviation * jax.random.normal(rng, extent, jnp.float32)
    if split:
        entries = entries * levels(rng, extent, split, -0.22, 0.18)
    return jnp.clip(entries, -most, most).astype(held_as)


def setup_inputs(seed: int = 0, part: int = 0) -> dict:
    splits = jax.random.split(jax.random.key(seed), 15)
    part_splits = jax.random.split(jax.random.fold_in(splits[14], part), 15)
    queries = draw_queries(jax.random.fold_in(jax.random.fold_in(splits[14], part), 71), part)
    new_keys = draw_new_keys(jax.random.fold_in(jax.random.fold_in(splits[14], part), 71), part)
    new_values = normal_values(part_splits[2], (TOKENS, KVH * HD), 1.0, 6.0, ((0, 16),))
    cache_keys = draw_cache_keys(jax.random.fold_in(jax.random.fold_in(splits[14], part), 71), part)
    cache_values = normal_values(part_splits[4], (REQUESTS * CACHE, KVH * HD), 1.0, 6.0, ((0, 16),))
    cache_lens = ragged_sizes(part_splits[5], REQUESTS, REQUESTS * CACHE * 5 // 8, CACHE, 2).astype(jnp.int32)
    residual = draw_residual(jax.random.fold_in(jax.random.fold_in(splits[14], part), 71), part)
    out_weight = normal_values(splits[7], (HEADS * HD, D), (HEADS * HD) ** -0.5, 0.09375, ((0, 16),))
    norm_gain = jnp.clip(1.0 + 0.15 * jax.random.normal(splits[8], (D,), jnp.float32), 0.25, 1.75)
    expert_ids_keys = jax.random.split(jax.random.fold_in(part_splits[9], 1), TOKENS // BLOCK)
    expert_ids_turns = jax.random.permutation(jax.random.fold_in(part_splits[9], 3), TOKENS // BLOCK)
    expert_ids = jax.vmap(lambda own, number: assign_block(jax.random.fold_in(part_splits[9], 2), own, number, BLOCK, EXPERTS, TOPK, CAP, 2))(expert_ids_keys, expert_ids_turns).reshape((TOKENS, TOPK))
    route_weights = jnp.clip(0.2 + 0.8 * jax.random.uniform(part_splits[10], (TOKENS, TOPK), jnp.float32) ** levels(part_splits[10], (TOKENS, TOPK), ((0, 16),), -0.2, 0.2), 0.2, 1.0)
    gate_weight = normal_values(splits[11], (EXPERTS, D, FF), D ** -0.5, 0.125, ((0, 16),))
    up_weight = normal_values(splits[12], (EXPERTS, D, FF), D ** -0.5, 0.125, ((0, 16),))
    down_weight = normal_values(splits[13], (EXPERTS, FF, D), FF ** -0.5, 0.3125, ((0, 16),))
    return dict(queries=queries, new_keys=new_keys, new_values=new_values, cache_keys=cache_keys, cache_values=cache_values, cache_lens=cache_lens, residual=residual, out_weight=out_weight, norm_gain=norm_gain, expert_ids=expert_ids, route_weights=route_weights, gate_weight=gate_weight, up_weight=up_weight, down_weight=down_weight)


def reference(queries, new_keys, new_values, cache_keys, cache_values, cache_lens, residual, out_weight, norm_gain, expert_ids, route_weights, gate_weight, up_weight, down_weight):
    group = HEADS // KVH
    scale = HD ** (-0.5)

    def one_request(operands):
        query_rows, key_new, value_new, key_cache, value_cache, length = operands
        key_all = jnp.concatenate([key_cache, key_new], 0).astype(jnp.float32).reshape(-1, KVH, HD)
        value_all = jnp.concatenate([value_cache, value_new], 0).astype(jnp.float32).reshape(-1, KVH, HD)
        shaped = query_rows.astype(jnp.float32).reshape(ROWS, KVH, group, HD)
        scores = jnp.einsum('rcgd,kcd->crgk', shaped, key_all) * scale
        cache_ok = jnp.arange(CACHE, dtype=jnp.int32)[None, :] < length
        cache_ok = jnp.broadcast_to(cache_ok, (ROWS, CACHE))
        new_ok = jnp.arange(ROWS, dtype=jnp.int32)[None, :] <= jnp.arange(ROWS, dtype=jnp.int32)[:, None]
        allowed = jnp.concatenate([cache_ok, new_ok], 1)
        scores = jnp.where(allowed[None, :, None, :], scores, -1e+30)
        weights = jax.nn.softmax(scores, axis=-1).astype(jnp.bfloat16)
        output = jnp.einsum('crgk,kcd->rcgd', weights.astype(jnp.float32), value_all).astype(jnp.bfloat16)
        return output.reshape(ROWS, HEADS * HD)
    attended = lax.map(one_request, (queries.reshape(REQUESTS, ROWS, -1), new_keys.reshape(REQUESTS, ROWS, -1), new_values.reshape(REQUESTS, ROWS, -1), cache_keys.reshape(REQUESTS, CACHE, -1), cache_values.reshape(REQUESTS, CACHE, -1), cache_lens))
    attended = attended.reshape(REQUESTS * ROWS, HEADS * HD)
    mixed = residual.astype(jnp.float32) + jnp.dot(attended, out_weight, preferred_element_type=jnp.float32)
    factor = lax.rsqrt(lax.optimization_barrier(jnp.mean(mixed * mixed, axis=-1, keepdims=True)) + 1e-06)
    normed = (mixed * factor * norm_gain).astype(jnp.bfloat16)
    blocks_all = REQUESTS * ROWS // BLOCK
    flat_ids = expert_ids.reshape(blocks_all, BLOCK * TOPK)
    matches = (flat_ids[:, :, None] == jnp.arange(EXPERTS, dtype=jnp.int32)[None, None, :]).astype(jnp.int32)
    ranking = lax.optimization_barrier(jnp.sum(jnp.cumsum(matches, axis=1) * matches, axis=-1)) - 1
    block_index = jnp.arange(blocks_all, dtype=jnp.int32)[:, None]
    slot_index = ((flat_ids * blocks_all + block_index) * CAP + ranking).reshape(-1).astype(jnp.int32)
    token_index = (block_index * BLOCK + jnp.arange(BLOCK * TOPK, dtype=jnp.int32)[None, :] // TOPK).reshape(-1).astype(jnp.int32)
    total_slots = EXPERTS * blocks_all * CAP
    source_row = jnp.zeros((total_slots,), jnp.int32).at[slot_index].set(token_index)
    filled = jnp.zeros((total_slots,), jnp.bool_).at[slot_index].set(True)

    def one_expert(operands):
        rows_index, used, gate_matrix, up_matrix, down_matrix = operands
        gathered = jnp.where(used[:, None], normed[rows_index], jnp.zeros((), jnp.bfloat16))
        gate_part = jnp.dot(gathered, gate_matrix, preferred_element_type=jnp.float32)
        up_part = jnp.dot(gathered, up_matrix, preferred_element_type=jnp.float32)
        hidden = (jax.nn.silu(gate_part) * up_part).astype(jnp.bfloat16)
        return jnp.dot(hidden, down_matrix, preferred_element_type=jnp.float32).astype(jnp.bfloat16)
    results = lax.map(one_expert, (source_row.reshape(EXPERTS, -1), filled.reshape(EXPERTS, -1), gate_weight, up_weight, down_weight))
    picked = results.reshape(total_slots, D)[slot_index].astype(jnp.float32).reshape(-1, TOPK, D)
    combined = lax.optimization_barrier(jnp.sum(picked * route_weights[:, :, None], axis=1))
    return (mixed + combined).astype(jnp.bfloat16)
```

```python
import functools
import math

import jax
import jax.numpy as jnp
import numpy as np
from jax import lax
from jax.experimental import pallas as pl
from jax.experimental.pallas import tpu as pltpu
from jax.sharding import PartitionSpec as P

HD = 128
KVH = 4
BLOCK = 64
BF = jnp.bfloat16
F32 = jnp.float32
ANY = pl.BlockSpec(memory_space=pl.ANY)
VMEM_LIMIT = 60 * 1024 * 1024


def attention_piece(lens, queries, new_keys, new_values, cache_keys, cache_values, kv):
    rows = queries.shape[0]
    cache = cache_keys.shape[0]
    width = queries.shape[1] // KVH
    pair = 2 * HD
    scale = HD ** (-0.5) * math.log2(math.e)

    def kernel(lens_ref, q_ref, kn_ref, vn_ref, kc_ref, vc_ref, o_ref, vca_ref, vna_ref, bias_ref):
        @pl.when(pl.program_id(0) == 0)
        def _():
            vca_ref[:, :HD] = vc_ref[...]
            vca_ref[:, HD:] = jnp.ones((cache, HD), BF)
            vna_ref[:, :HD] = vn_ref[...]
            vna_ref[:, HD:] = jnp.ones((rows, HD), BF)
            at = lax.broadcasted_iota(jnp.int32, (8, cache), 1)
            bias_ref[...] = jnp.where(at < lens_ref[0], 0.0, -1e30).astype(F32)

        q = q_ref[...]
        q2 = jnp.concatenate([q[:, :HD], q[:, HD:]], axis=0)
        dims = (((1,), (1,)), ((), ()))
        sc = lax.dot_general(q2, kc_ref[...], dims, preferred_element_type=F32)
        sn = lax.dot_general(q2, kn_ref[...], dims, preferred_element_type=F32)
        sc = sc + bias_ref[0:1, :]
        row = lax.broadcasted_iota(jnp.int32, (2 * rows, rows), 0)
        row = jnp.where(row >= rows, row - rows, row)
        col = lax.broadcasted_iota(jnp.int32, (2 * rows, rows), 1)
        sn = jnp.where(col <= row, sn, -1e30)
        top = jnp.maximum(
            jnp.max(sc, axis=1, keepdims=True), jnp.max(sn, axis=1, keepdims=True)
        )
        pc = jnp.exp2((sc - top) * scale).astype(BF)
        pn = jnp.exp2((sn - top) * scale).astype(BF)
        acc = jnp.dot(pc, vca_ref[...], preferred_element_type=F32)
        acc = acc + jnp.dot(pn, vna_ref[...], preferred_element_type=F32)
        out = (acc[:, :HD] / acc[:, HD:]).astype(BF)
        o_ref[:, :HD] = out[:rows]
        o_ref[:, HD:] = out[rows:]

    steps = width // pair
    keys = cache + rows
    return pl.pallas_call(
        kernel,
        name="attend",
        out_shape=jax.ShapeDtypeStruct((rows, width), BF),
        grid_spec=pltpu.PrefetchScalarGridSpec(
            num_scalar_prefetch=1,
            grid=(steps,),
            in_specs=[
                pl.BlockSpec((rows, pair), lambda i, _: (0, kv * steps + i)),
                pl.BlockSpec((rows, HD), lambda i, _: (0, kv)),
                pl.BlockSpec((rows, HD), lambda i, _: (0, kv)),
                pl.BlockSpec((cache, HD), lambda i, _: (0, kv)),
                pl.BlockSpec((cache, HD), lambda i, _: (0, kv)),
            ],
            out_specs=pl.BlockSpec((rows, pair), lambda i, _: (0, i)),
            scratch_shapes=[
                pltpu.VMEM((cache, 2 * HD), BF),
                pltpu.VMEM((rows, 2 * HD), BF),
                pltpu.VMEM((8, cache), F32),
            ],
        ),
        compiler_params=pltpu.CompilerParams(vmem_limit_bytes=VMEM_LIMIT),
        cost_estimate=pl.CostEstimate(
            flops=4 * rows * width * keys * 2,
            transcendentals=rows * (width // HD) * keys,
            bytes_accessed=4 * keys * HD + 4 * rows * width,
        ),
    )(lens, queries, new_keys, new_values, cache_keys, cache_values)


def project(table, pieces, weights, tail_a, tail_b, half_rows):
    devices = len(pieces)
    rows, width = pieces[0][0].shape
    flat = [p for device in pieces for p in device]
    blocks = len(weights) + 1
    kblock, cols = weights[0].shape
    count = len(flat)

    def kernel(*refs):
        table_ref = refs[0]
        piece_refs = refs[1 : 1 + count]
        weight_refs = refs[1 + count : 1 + count + blocks + 1]
        outs = refs[2 + count + blocks : 2 + count + blocks + devices]
        a_ref, w_ref, a_sem, w_sem = refs[2 + count + blocks + devices :]
        copies = []
        for d in range(devices):
            for j in range(KVH):
                at = d * KVH + j
                copies.append(
                    pltpu.make_async_copy(
                        piece_refs[at],
                        a_ref.at[pl.ds(d * rows, rows), pl.ds(j * width, width)],
                        a_sem.at[at],
                    )
                )
        wcopies = []
        for s in range(blocks - 1):
            wcopies.append(
                [pltpu.make_async_copy(weight_refs[s], w_ref.at[s], w_sem.at[s])]
            )
        wcopies.append(
            [
                pltpu.make_async_copy(
                    weight_refs[blocks - 1],
                    w_ref.at[blocks - 1, pl.ds(0, half_rows)],
                    w_sem.at[blocks - 1],
                ),
                pltpu.make_async_copy(
                    weight_refs[blocks],
                    w_ref.at[blocks - 1, pl.ds(half_rows, half_rows)],
                    w_sem.at[blocks],
                ),
            ]
        )
        for copy in copies:
            copy.start()
        for group in wcopies:
            for copy in group:
                copy.start()
        for copy in copies:
            copy.wait()
        acc = jnp.zeros((devices * rows, cols), F32)
        for s in range(blocks):
            for copy in wcopies[s]:
                copy.wait()
            for half in range(2):
                base = pl.multiple_of(table_ref[2 * s + half], half_rows)
                acc = acc + jnp.dot(
                    a_ref[:, pl.ds(base, half_rows)],
                    w_ref[s, half * half_rows : (half + 1) * half_rows, :],
                    preferred_element_type=F32,
                )
        for d in range(devices):
            outs[d][...] = acc[d * rows : (d + 1) * rows].astype(BF)

    vm = pl.BlockSpec(memory_space=pltpu.VMEM)
    return pl.pallas_call(
        kernel,
        name="project",
        out_shape=[jax.ShapeDtypeStruct((rows, cols), BF)] * devices,
        in_specs=[pl.BlockSpec(memory_space=pltpu.SMEM)] + [ANY] * (count + blocks + 1),
        out_specs=[vm] * devices,
        scratch_shapes=[
            pltpu.VMEM((devices * rows, KVH * width), BF),
            pltpu.VMEM((blocks, kblock, cols), BF),
            pltpu.SemaphoreType.DMA((count,)),
            pltpu.SemaphoreType.DMA((blocks + 1,)),
        ],
        compiler_params=pltpu.CompilerParams(vmem_limit_bytes=VMEM_LIMIT),
        cost_estimate=pl.CostEstimate(
            flops=2 * devices * rows * blocks * kblock * cols,
            transcendentals=0,
            bytes_accessed=2 * (devices * rows * KVH * width + blocks * kblock * cols),
        ),
    )(table, *flat, *weights, tail_a, tail_b)


def mix_norm(table, residual, gain, pieces):
    rows, width = residual.shape
    cols = pieces[0].shape[1]

    def kernel(table_ref, residual_ref, gain_ref, *refs):
        piece_refs = refs[: len(pieces)]
        mixed_ref, normed_ref = refs[len(pieces) :]
        total = jnp.zeros((rows, 1), F32)
        for d in range(len(pieces)):
            at = pl.ds(pl.multiple_of(table_ref[d], cols), cols)
            part = residual_ref[:, at].astype(F32) + piece_refs[d][...].astype(F32)
            mixed_ref[:, at] = part
            total = total + jnp.sum(part * part, axis=1, keepdims=True)
        factor = lax.rsqrt(total / width + 1e-6)
        normed_ref[...] = (mixed_ref[...] * factor * gain_ref[...]).astype(BF)

    vm = pl.BlockSpec(memory_space=pltpu.VMEM)
    return pl.pallas_call(
        kernel,
        name="mixnorm",
        out_shape=[
            jax.ShapeDtypeStruct((rows, width), F32),
            jax.ShapeDtypeStruct((rows, width), BF),
        ],
        in_specs=[pl.BlockSpec(memory_space=pltpu.SMEM)] + [vm] * (2 + len(pieces)),
        out_specs=[vm, vm],
        compiler_params=pltpu.CompilerParams(vmem_limit_bytes=VMEM_LIMIT),
        cost_estimate=pl.CostEstimate(
            flops=6 * rows * width, transcendentals=rows, bytes_accessed=10 * rows * width
        ),
    )(table, residual, gain.reshape(1, -1), *pieces)


def experts(slots, shares, blocks, gate, up, down, capacity):
    local, width, hidden = gate.shape
    sizes = [b.shape[0] for b in blocks]
    starts = [int(v) for v in np.cumsum([0] + sizes)]
    tokens = starts[-1]
    group_blocks = 1
    while group_blocks * capacity % 16 or group_blocks * BLOCK < 256:
        group_blocks *= 2
    span = group_blocks * BLOCK
    per = group_blocks * capacity
    groups = tokens // span
    count = len(blocks)

    def kernel(slots_ref, shares_ref, *refs):
        block_refs = refs[:count]
        gate_ref, up_ref, down_ref = refs[count : count + 3]
        outs = refs[count + 3 : 2 * count + 3]
        x_ref, g_ref, u_ref, d_ref, xs_ref, y_ref, x_sem, w_sem, o_sem = refs[2 * count + 3 :]
        o_ref = x_ref
        xcopies = [
            pltpu.make_async_copy(
                block_refs[i], x_ref.at[pl.ds(starts[i], sizes[i])], x_sem.at[i]
            )
            for i in range(count)
        ]
        wcopies = []
        for e in range(local):
            wcopies.append(
                [
                    pltpu.make_async_copy(src.at[e], dst.at[e], w_sem.at[e, k])
                    for k, (src, dst) in enumerate(
                        [(gate_ref, g_ref), (up_ref, u_ref), (down_ref, d_ref)]
                    )
                ]
            )
        for copy in xcopies:
            copy.start()
        for trio in wcopies:
            for copy in trio:
                copy.start()
        for copy in xcopies:
            copy.wait()

        at = lax.broadcasted_iota(jnp.int32, (per, span), 0)

        def picks(g):
            return [
                slots_ref[e : e + 1, g * span : (g + 1) * span] == at for e in range(local)
            ]

        for g in range(groups):
            chosen = jnp.concatenate([p.astype(F32) for p in picks(g)], 0).astype(BF)
            picked = jnp.dot(
                chosen, x_ref[g * span : (g + 1) * span, :], preferred_element_type=F32
            ).astype(BF)
            for e in range(local):
                xs_ref[e, g * per : (g + 1) * per, :] = picked[e * per : (e + 1) * per]
        for e in range(local):
            for copy in wcopies[e]:
                copy.wait()
            rows = xs_ref[e]
            gate_part = jnp.dot(rows, g_ref[e], preferred_element_type=F32)
            up_part = jnp.dot(rows, u_ref[e], preferred_element_type=F32)
            inner = (gate_part / (1.0 + jnp.exp(-gate_part)) * up_part).astype(BF)
            result = jnp.dot(inner, d_ref[e], preferred_element_type=F32)
            for g in range(groups):
                chosen = slots_ref[e : e + 1, g * span : (g + 1) * span] == at
                share = jnp.sum(
                    jnp.where(chosen, shares_ref[e : e + 1, g * span : (g + 1) * span], 0.0),
                    axis=1,
                    keepdims=True,
                )
                part = result[g * per : (g + 1) * per] * share
                y_ref[g, e * per : (e + 1) * per, :] = part.astype(BF)
        ocopies = [
            pltpu.make_async_copy(
                o_ref.at[pl.ds(starts[i], sizes[i])], outs[i], o_sem.at[i]
            )
            for i in range(count)
        ]
        done = 0
        for g in range(groups):
            chosen = jnp.concatenate([p.astype(F32) for p in picks(g)], 0).astype(BF)
            o_ref[g * span : (g + 1) * span, :] = lax.dot_general(
                chosen, y_ref[g], (((0,), (0,)), ((), ())), preferred_element_type=F32
            ).astype(BF)
            while done < count and starts[done + 1] <= (g + 1) * span:
                ocopies[done].start()
                done += 1
        for copy in ocopies:
            copy.wait()

    vm = pl.BlockSpec(memory_space=pltpu.VMEM)
    return pl.pallas_call(
        kernel,
        name="experts",
        out_shape=[jax.ShapeDtypeStruct(b.shape, BF) for b in blocks],
        in_specs=[vm, vm] + [ANY] * (count + 3),
        out_specs=[ANY] * count,
        scratch_shapes=[
            pltpu.VMEM((tokens, width), BF),
            pltpu.VMEM(gate.shape, BF),
            pltpu.VMEM(up.shape, BF),
            pltpu.VMEM(down.shape, BF),
            pltpu.VMEM((local, groups * per, width), BF),
            pltpu.VMEM((groups, local * per, width), BF),
            pltpu.SemaphoreType.DMA((count,)),
            pltpu.SemaphoreType.DMA((local, 3)),
            pltpu.SemaphoreType.DMA((count,)),
        ],
        compiler_params=pltpu.CompilerParams(vmem_limit_bytes=VMEM_LIMIT),
        cost_estimate=pl.CostEstimate(
            flops=6 * local * groups * per * width * hidden,
            transcendentals=local * groups * per * hidden,
            bytes_accessed=6 * local * width * hidden + 4 * tokens * width,
        ),
    )(slots, shares, *blocks, gate, up, down)


def slot_tables(ids, shares, first, local, capacity, per_group):
    tokens = ids.shape[1]
    expert = (first + jnp.arange(local)).astype(ids.dtype)
    hit = ids[None] == expert[:, None, None]
    share = jnp.sum(jnp.where(hit, shares[None], 0.0), axis=1)
    match = jnp.any(hit, axis=1)
    blocks = match.reshape(local * (tokens // BLOCK), BLOCK)
    before = jnp.asarray(np.triu(np.ones((BLOCK, BLOCK)), 1), BF)
    rank = jnp.dot(blocks.astype(BF), before, preferred_element_type=F32)
    rank = rank.astype(jnp.int32).reshape(local, tokens)
    place = (jnp.arange(tokens) // BLOCK % per_group) * capacity
    return jnp.where(match, rank + place[None], -1), share


def solution(mesh):
    groups = mesh.shape["groups"]
    devices = mesh.shape["tok"]
    cores = 2
    chips = devices // cores
    layer = max(1, 4 // groups)
    if chips % layer:
        layer = 1
    levels = chips // layer
    if layer == 2:
        order = [z * 2 for z in range(levels)] + [z * 2 + 1 for z in reversed(range(levels))]
    else:
        order = list(range(chips))
    position = [order.index(chip) for chip in range(chips)]
    reach = chips // 2

    def shift(step):
        pairs = []
        for at, chip in enumerate(order):
            for core in range(cores):
                pairs.append((chip * cores + core, order[(at + step) % chips] * cores + core))
        return pairs

    forward, backward = shift(1), shift(-1)
    swap = [(i, i ^ 1) for i in range(devices)]
    across = [(g, g ^ 1) for g in range(groups)]
    diagonal = [
        (g * devices + t, (g ^ 1) * devices + (t ^ 1))
        for g in range(groups)
        for t in range(devices)
    ]

    def to_forward(v):
        return lax.ppermute(v, "tok", forward)

    def to_backward(v):
        return lax.ppermute(v, "tok", backward)

    def to_sibling(v):
        return lax.ppermute(v, "tok", swap)

    def to_across(v):
        return lax.ppermute(v, "groups", across)

    def to_diagonal(v):
        return lax.ppermute(v, ("groups", "tok"), diagonal)

    def ring_gather(block):
        found = {0: block}
        ahead = back = block
        for step in range(1, reach):
            ahead = to_forward(ahead)
            back = to_backward(back)
            found[chips - step] = ahead
            found[step] = back
        middle = block.shape[0] // 2
        return found, to_forward(ahead[:middle]), to_backward(back[middle:])

    def ring_reduce(parts, low, high):
        ahead = to_forward(low)
        back = to_backward(high)
        middle = low.shape[0]
        for step in range(reach - 1, 0, -1):
            one, two = parts[step], parts[chips - step]
            if step == reach - 1:
                one = jnp.concatenate([add(one[:middle], ahead), one[middle:]], 0)
                two = jnp.concatenate([two[:middle], add(two[middle:], back)], 0)
            else:
                one, two = add(one, ahead), add(two, back)
            ahead, back = to_forward(one), to_backward(two)
        return ahead, back

    def add(*values):
        total = values[0].astype(F32)
        for value in values[1:]:
            total = total + value.astype(F32)
        return total.astype(BF)

    def body(
        queries,
        new_keys,
        new_values,
        cache_keys,
        cache_values,
        cache_lens,
        residual,
        out_weight,
        norm_gain,
        expert_ids,
        route_weights,
        gate_weight,
        up_weight,
        down_weight,
    ):
        rows, width = residual.shape
        local = gate_weight.shape[0]
        top = expert_ids.shape[1]
        capacity = max(2, BLOCK * top * 3 // (2 * local * devices))
        half_rows = out_weight.shape[0]
        cols = width // 4
        me = lax.axis_index("tok")
        core = me % cores
        quarter = (lax.axis_index("groups") % 2) * 2 + core
        mine = jnp.asarray(position, jnp.int32)[me // cores]

        meta = jnp.concatenate([expert_ids.T.astype(F32), route_weights.T], 0)
        metas = [meta] + [lax.ppermute(meta, "tok", shift(-s)) for s in range(1, chips)]
        meta = jnp.concatenate(metas, 1)
        meta = jnp.concatenate([meta, to_sibling(meta)], 1)
        per_group = 1
        while per_group * capacity % 16 or per_group * BLOCK < 256:
            per_group *= 2
        slots, shares = slot_tables(
            meta[:top].astype(jnp.int32), meta[top:], me * local, local, capacity, per_group
        )

        own = lax.dynamic_slice_in_dim(out_weight, quarter * cols, cols, 1)
        other = to_sibling(lax.dynamic_slice_in_dim(out_weight, (quarter ^ 1) * cols, cols, 1))
        wfound, wlow, whigh = ring_gather(jnp.concatenate([own, other], 0))

        pieces = [[], [], [], []]
        for kv in range(KVH):
            piece = attention_piece(
                cache_lens, queries, new_keys, new_values, cache_keys, cache_values, kv
            )
            far = to_across(piece)
            pieces[0].append(piece)
            pieces[1].append(to_sibling(piece))
            pieces[2].append(far)
            pieces[3].append(to_sibling(far))

        offsets = [0] + [v for s in range(1, reach) for v in (s, chips - s)]
        chip_at = jnp.asarray(order, jnp.int32)[
            (mine + jnp.asarray(offsets + [reach], jnp.int32)) % chips
        ]
        first = chip_at * (cores * half_rows)
        table = jnp.stack([first + core * half_rows, first + (1 - core) * half_rows], 1)
        products = project(
            table.reshape(-1).astype(jnp.int32),
            pieces,
            [wfound[o] for o in offsets],
            wlow,
            whigh,
            half_rows,
        )
        returned = [
            products[0],
            to_sibling(products[1]),
            to_across(products[2]),
            to_diagonal(products[3]),
        ]
        columns = (quarter ^ jnp.arange(4)).astype(jnp.int32) * cols
        mixed, normed = mix_norm(columns, residual, norm_gain, returned)

        found, low, high = ring_gather(normed)
        near = [found[o] for o in range(reach)] + [low, high]
        near += [found[o] for o in range(reach + 1, chips)]
        blocks = near + [to_sibling(v) for v in near]
        sums = experts(
            slots, shares, blocks, gate_weight, up_weight, down_weight, capacity
        )
        count = len(near)
        crossed = [to_sibling(v) for v in sums[count:]]
        joined = [add(a, b) for a, b in zip(sums[1:count], crossed[1:])]
        joined = [None] + joined
        parts = {}
        for o in range(1, reach):
            parts[o] = joined[o]
            parts[chips - o] = joined[count - o]
        ahead, back = ring_reduce(parts, joined[reach], joined[reach + 1])
        final = mixed + (
            sums[0].astype(F32)
            + crossed[0].astype(F32)
            + ahead.astype(F32)
            + back.astype(F32)
        )
        return final.astype(BF)

    placed = (
        P(("groups", "tok"), None),
        P(("groups", "tok"), None),
        P(("groups", "tok"), None),
        P(("groups", "tok"), None),
        P(("groups", "tok"), None),
        P(("groups", "tok")),
        P(("groups", "tok"), None),
        P("tok", None),
        P(),
        P(("groups", "tok"), None),
        P(("groups", "tok"), None),
        P("tok", None, None),
        P("tok", None, None),
        P("tok", None, None),
    )
    return jax.shard_map(
        body, mesh=mesh, in_specs=placed, out_specs=P(("groups", "tok"), None), check_vma=False
    )
```

```python
import functools
import math

import jax
import jax.numpy as jnp
import numpy as np
from jax import lax
from jax.experimental import pallas as pl
from jax.experimental.pallas import tpu as pltpu
from jax.sharding import PartitionSpec as P

HD = 128
KVH = 4
BLOCK = 64
BF = jnp.bfloat16
F32 = jnp.float32
ANY = pl.BlockSpec(memory_space=pl.ANY)
VMEM_LIMIT = 60 * 1024 * 1024


def attention_piece(lens, queries, new_keys, new_values, cache_keys, cache_values, kv):
    rows = queries.shape[0]
    cache = cache_keys.shape[0]
    width = queries.shape[1] // KVH
    pair = 2 * HD
    scale = HD ** (-0.5) * math.log2(math.e)

    def kernel(lens_ref, q_ref, kn_ref, vn_ref, kc_ref, vc_ref, o_ref, va_ref, bias_ref):
        va_ref[:cache, :HD] = vc_ref[...]
        va_ref[cache:, :HD] = vn_ref[...]
        va_ref[:, HD:] = jnp.ones((cache + rows, HD), BF)
        at = lax.broadcasted_iota(jnp.int32, (8, cache), 1)
        bias_ref[...] = jnp.where(at < lens_ref[0], 0.0, -1e30).astype(F32)
        row = lax.broadcasted_iota(jnp.int32, (2 * rows, rows), 0)
        row = jnp.where(row >= rows, row - rows, row)
        col = lax.broadcasted_iota(jnp.int32, (2 * rows, rows), 1)
        dims = (((1,), (1,)), ((), ()))
        for at in range(width // pair):
            lo, mid, hi = at * pair, at * pair + HD, (at + 1) * pair
            q2 = jnp.concatenate([q_ref[:, lo:mid], q_ref[:, mid:hi]], axis=0)
            sc = lax.dot_general(q2, kc_ref[...], dims, preferred_element_type=F32)
            sn = lax.dot_general(q2, kn_ref[...], dims, preferred_element_type=F32)
            sc = sc + bias_ref[0:1, :]
            sn = jnp.where(col <= row, sn, -1e30)
            top = jnp.maximum(
                jnp.max(sc, axis=1, keepdims=True), jnp.max(sn, axis=1, keepdims=True)
            )
            pc = jnp.exp2((sc - top) * scale).astype(BF)
            pn = jnp.exp2((sn - top) * scale).astype(BF)
            acc = jnp.dot(pc, va_ref[:cache], preferred_element_type=F32)
            acc = acc + jnp.dot(pn, va_ref[cache:], preferred_element_type=F32)
            out = (acc[:, :HD] / acc[:, HD:]).astype(BF)
            o_ref[:, lo:mid] = out[:rows]
            o_ref[:, mid:hi] = out[rows:]

    keys = cache + rows
    return pl.pallas_call(
        kernel,
        name="attend",
        out_shape=jax.ShapeDtypeStruct((rows, width), BF),
        grid_spec=pltpu.PrefetchScalarGridSpec(
            num_scalar_prefetch=1,
            grid=(1,),
            in_specs=[
                pl.BlockSpec((rows, width), lambda i, _: (0, kv)),
                pl.BlockSpec((rows, HD), lambda i, _: (0, kv)),
                pl.BlockSpec((rows, HD), lambda i, _: (0, kv)),
                pl.BlockSpec((cache, HD), lambda i, _: (0, kv)),
                pl.BlockSpec((cache, HD), lambda i, _: (0, kv)),
            ],
            out_specs=pl.BlockSpec((rows, width), lambda i, _: (0, 0)),
            scratch_shapes=[
                pltpu.VMEM((keys, 2 * HD), BF),
                pltpu.VMEM((8, cache), F32),
            ],
        ),
        compiler_params=pltpu.CompilerParams(vmem_limit_bytes=VMEM_LIMIT),
        cost_estimate=pl.CostEstimate(
            flops=4 * rows * width * keys * 2,
            transcendentals=rows * (width // HD) * keys,
            bytes_accessed=4 * keys * HD + 4 * rows * width,
        ),
    )(lens, queries, new_keys, new_values, cache_keys, cache_values)


def project(table, pieces, weights):
    devices = len(pieces)
    rows, width = pieces[0][0].shape
    flat = [p for device in pieces for p in device]
    count = len(flat)
    blocks = len(weights)
    depth, cols = weights[0].shape
    half = rows // 2

    def kernel(*refs):
        table_ref = refs[0]
        piece_refs = refs[1 : 1 + count]
        weight_refs = refs[1 + count : 1 + count + blocks]
        outs = refs[1 + count + blocks : 1 + count + blocks + 2 * devices]
        a_ref, w_ref, a_sem, w_sem = refs[1 + count + blocks + 2 * devices :]
        copies = []
        for d in range(devices):
            for j in range(KVH):
                at = d * KVH + j
                copies.append(
                    pltpu.make_async_copy(
                        piece_refs[at],
                        a_ref.at[pl.ds(d * rows, rows), pl.ds(j * width, width)],
                        a_sem.at[at],
                    )
                )
        wcopies = [
            pltpu.make_async_copy(weight_refs[s], w_ref.at[s], w_sem.at[s])
            for s in range(blocks)
        ]
        for copy in copies + wcopies:
            copy.start()
        for copy in copies:
            copy.wait()
        acc = jnp.zeros((devices * rows, cols), F32)
        for s in range(blocks):
            wcopies[s].wait()
            base = pl.multiple_of(table_ref[s], depth)
            acc = acc + jnp.dot(
                a_ref[:, pl.ds(base, depth)], w_ref[s], preferred_element_type=F32
            )
        for d in range(devices):
            for k in range(2):
                outs[2 * d + k][...] = acc[d * rows + k * half : d * rows + (k + 1) * half].astype(
                    BF
                )

    vm = pl.BlockSpec(memory_space=pltpu.VMEM)
    out = pl.pallas_call(
        kernel,
        name="project",
        out_shape=[jax.ShapeDtypeStruct((half, cols), BF)] * (2 * devices),
        in_specs=[pl.BlockSpec(memory_space=pltpu.SMEM)] + [ANY] * (count + blocks),
        out_specs=[vm] * (2 * devices),
        scratch_shapes=[
            pltpu.VMEM((devices * rows, KVH * width), BF),
            pltpu.VMEM((blocks, depth, cols), BF),
            pltpu.SemaphoreType.DMA((count,)),
            pltpu.SemaphoreType.DMA((blocks,)),
        ],
        compiler_params=pltpu.CompilerParams(vmem_limit_bytes=VMEM_LIMIT),
        cost_estimate=pl.CostEstimate(
            flops=2 * devices * rows * blocks * depth * cols,
            transcendentals=0,
            bytes_accessed=2 * (devices * rows * KVH * width + blocks * depth * cols),
        ),
    )(table, *flat, *weights)
    return [out[2 * d : 2 * d + 2] for d in range(devices)]


def mix_norm(table, residual, gain, pieces, part):
    rows, width = residual.shape[0] // 2, residual.shape[1]
    cols = pieces[0].shape[1]

    def kernel(table_ref, residual_ref, gain_ref, *refs):
        piece_refs = refs[: len(pieces)]
        mixed_ref, normed_ref = refs[len(pieces) :]
        total = jnp.zeros((rows, 1), F32)
        for d in range(len(pieces)):
            at = pl.ds(pl.multiple_of(table_ref[d], cols), cols)
            mixed = residual_ref[:, at].astype(F32) + piece_refs[d][...].astype(F32)
            mixed_ref[:, at] = mixed
            total = total + jnp.sum(mixed * mixed, axis=1, keepdims=True)
        factor = lax.rsqrt(total / width + 1e-6)
        normed_ref[...] = (mixed_ref[...] * factor * gain_ref[...]).astype(BF)

    def whole(shape):
        return pl.BlockSpec(shape, lambda i, _: (0, 0))

    return pl.pallas_call(
        kernel,
        name="mixnorm",
        out_shape=[
            jax.ShapeDtypeStruct((rows, width), F32),
            jax.ShapeDtypeStruct((rows, width), BF),
        ],
        grid_spec=pltpu.PrefetchScalarGridSpec(
            num_scalar_prefetch=1,
            grid=(1,),
            in_specs=[pl.BlockSpec((rows, width), lambda i, _: (part, 0)), whole((1, width))]
            + [whole((rows, cols))] * len(pieces),
            out_specs=[whole((rows, width)), whole((rows, width))],
        ),
        compiler_params=pltpu.CompilerParams(vmem_limit_bytes=VMEM_LIMIT),
        cost_estimate=pl.CostEstimate(
            flops=6 * rows * width, transcendentals=rows, bytes_accessed=10 * rows * width
        ),
    )(table, residual, gain.reshape(1, -1), *pieces)


def slot_tables(who, first, meta, local, top, capacity, per_group):
    devices, _, rows = meta.shape
    tokens = devices * rows

    def kernel(who_ref, first_ref, meta_ref, slots_ref, shares_ref):
        i = lax.broadcasted_iota(jnp.int32, (rows, rows), 0)
        j = lax.broadcasted_iota(jnp.int32, (rows, rows), 1)
        before = ((i < j) & (i // BLOCK == j // BLOCK)).astype(F32).astype(BF)
        inside = lax.broadcasted_iota(jnp.int32, (1, rows), 1) // BLOCK
        for d in range(devices):
            part = meta_ref[who_ref[d]]
            ids = part[:top].astype(jnp.int32)
            match, share = [], []
            for e in range(local):
                hit = ids == first_ref[0] + e
                share.append(jnp.sum(jnp.where(hit, part[top:], 0.0), axis=0, keepdims=True))
                match.append(jnp.max(hit.astype(F32), axis=0, keepdims=True))
            match = jnp.concatenate(match, 0)
            rank = jnp.dot(match.astype(BF), before, preferred_element_type=F32)
            place = (d * (rows // BLOCK) + inside) % per_group * capacity
            at = pl.ds(d * rows, rows)
            slots_ref[:, at] = jnp.where(match > 0, rank.astype(jnp.int32) + place, -1)
            shares_ref[:, at] = jnp.concatenate(share, 0)

    sm = pl.BlockSpec(memory_space=pltpu.SMEM)
    vm = pl.BlockSpec(memory_space=pltpu.VMEM)
    return pl.pallas_call(
        kernel,
        name="tables",
        out_shape=[
            jax.ShapeDtypeStruct((local, tokens), jnp.int32),
            jax.ShapeDtypeStruct((local, tokens), F32),
        ],
        in_specs=[sm, sm, vm],
        out_specs=[vm, vm],
    )(who, first, meta)


def chosen_rows(slots_ref, group, span, per, local):
    at = lax.broadcasted_iota(jnp.int32, (per, span), 0)
    return jnp.concatenate(
        [
            (slots_ref[e : e + 1, group * span : (group + 1) * span] == at).astype(F32)
            for e in range(local)
        ],
        0,
    ).astype(BF)


def select_rows(slots, blocks, groups, span, per):
    local = slots.shape[0]
    width = blocks[0].shape[1]
    sizes = [b.shape[0] for b in blocks]
    starts = [int(v) for v in np.cumsum([0] + sizes)]
    count = len(blocks)

    def kernel(slots_ref, *refs):
        block_refs, out_ref, x_ref, sem = refs[:count], refs[count], refs[count + 1], refs[count + 2]
        copies = [
            pltpu.make_async_copy(block_refs[i], x_ref.at[pl.ds(starts[i], sizes[i])], sem.at[i])
            for i in range(count)
        ]
        for copy in copies:
            copy.start()
        done = 0
        for k, g in enumerate(groups):
            while done < count and starts[done] < (k + 1) * span:
                copies[done].wait()
                done += 1
            chosen = chosen_rows(slots_ref, g, span, per, local)
            picked = jnp.dot(
                chosen, x_ref[k * span : (k + 1) * span, :], preferred_element_type=F32
            ).astype(BF)
            for e in range(local):
                out_ref[e, k * per : (k + 1) * per, :] = picked[e * per : (e + 1) * per]

    vm = pl.BlockSpec(memory_space=pltpu.VMEM)
    return pl.pallas_call(
        kernel,
        name="select",
        out_shape=jax.ShapeDtypeStruct((local, len(groups) * per, width), BF),
        in_specs=[vm] + [ANY] * count,
        out_specs=vm,
        scratch_shapes=[
            pltpu.VMEM((len(groups) * span, width), BF),
            pltpu.SemaphoreType.DMA((count,)),
        ],
        compiler_params=pltpu.CompilerParams(vmem_limit_bytes=VMEM_LIMIT),
        cost_estimate=pl.CostEstimate(
            flops=2 * local * len(groups) * per * span * width,
            transcendentals=0,
            bytes_accessed=2 * width * len(groups) * (span + local * per),
        ),
    )(slots, *blocks)


def experts(slots, shares, picked, blocks, gate, up, down, span, per):
    local, width, hidden = gate.shape
    sizes = [b.shape[0] for b in blocks]
    starts = [int(v) for v in np.cumsum([0] + sizes)]
    count = len(blocks)
    parts = len(picked)
    lengths = [p.shape[1] for p in picked]
    begins = [int(v) for v in np.cumsum([0] + lengths)]
    others = begins[-1] // per
    slots_all = begins[-1] + per
    outs_n = 3 * (count // 4)
    half = sizes[0]

    def kernel(slots_ref, shares_ref, *refs):
        picked_refs = refs[:parts]
        block_refs = refs[parts : parts + count]
        gate_ref, up_ref, down_ref = refs[parts + count : parts + count + 3]
        rest = refs[parts + count + 3 :]
        y_out = rest[0]
        outs = rest[1 : 1 + outs_n]
        x_ref, gu_ref, d_ref, xs_ref, y_ref, x_sem, p_sem, w_sem, y_sem = rest[1 + outs_n :]
        xcopies = [
            pltpu.make_async_copy(block_refs[i], x_ref.at[pl.ds(starts[i], sizes[i])], x_sem.at[i])
            for i in range(count)
        ]
        pcopies = [
            pltpu.make_async_copy(
                picked_refs[i], xs_ref.at[:, pl.ds(begins[i], lengths[i])], p_sem.at[i]
            )
            for i in range(parts)
        ]
        wcopies = [
            [
                pltpu.make_async_copy(
                    gate_ref.at[e], gu_ref.at[e, :, pl.ds(0, hidden)], w_sem.at[e, 0]
                ),
                pltpu.make_async_copy(
                    up_ref.at[e], gu_ref.at[e, :, pl.ds(hidden, hidden)], w_sem.at[e, 1]
                ),
                pltpu.make_async_copy(down_ref.at[e], d_ref.at[e], w_sem.at[e, 2]),
            ]
            for e in range(local)
        ]
        for copy in xcopies + wcopies[0] + pcopies:
            copy.start()
        for trio in wcopies[1:]:
            for copy in trio:
                copy.start()
        for copy in xcopies:
            copy.wait()
        chosen = chosen_rows(slots_ref, others, span, per, local)
        last = jnp.dot(chosen, x_ref[...], preferred_element_type=F32).astype(BF)
        for copy in pcopies:
            copy.wait()
        for e in range(local):
            xs_ref[e, begins[-1] :, :] = last[e * per : (e + 1) * per]
        at = lax.broadcasted_iota(jnp.int32, (per, span), 0)
        ycopies = []
        for e in range(local):
            for copy in wcopies[e]:
                copy.wait()
            both = jnp.dot(xs_ref[e], gu_ref[e], preferred_element_type=F32)
            gate_part, up_part = both[:, :hidden], both[:, hidden:]
            inner = (gate_part / (1.0 + jnp.exp(-gate_part)) * up_part).astype(BF)
            share = []
            for g in range(others + 1):
                here = slots_ref[e : e + 1, g * span : (g + 1) * span] == at
                share.append(
                    jnp.sum(
                        jnp.where(here, shares_ref[e : e + 1, g * span : (g + 1) * span], 0.0),
                        axis=1,
                        keepdims=True,
                    )
                )
            result = jnp.dot(inner, d_ref[e], preferred_element_type=F32)
            result = (result * jnp.concatenate(share, 0)).astype(BF)
            for g in range(others + 1):
                y_ref[g, e * per : (e + 1) * per, :] = result[g * per : (g + 1) * per]
            ycopies.append(
                pltpu.make_async_copy(
                    y_ref.at[pl.ds(0, others), pl.ds(e * per, per)],
                    y_out.at[:, pl.ds(e * per, per)],
                    y_sem.at[e],
                )
            )
            ycopies[-1].start()
        total = lax.dot_general(
            chosen, y_ref[others], (((0,), (0,)), ((), ())), preferred_element_type=F32
        ).astype(BF)
        spread(outs, total, half)
        for copy in ycopies:
            copy.wait()

    vm = pl.BlockSpec(memory_space=pltpu.VMEM)
    shapes = [(others, local * per, width)] + [(half, width), (half, width), (2 * half, width)] * (
        count // 4
    )
    out = pl.pallas_call(
        kernel,
        name="experts",
        out_shape=[jax.ShapeDtypeStruct(s, BF) for s in shapes],
        in_specs=[vm, vm] + [ANY] * (parts + count + 3),
        out_specs=[ANY] + [vm] * outs_n,
        scratch_shapes=[
            pltpu.VMEM((span, width), BF),
            pltpu.VMEM((local, width, 2 * hidden), BF),
            pltpu.VMEM(down.shape, BF),
            pltpu.VMEM((local, slots_all, width), BF),
            pltpu.VMEM((others + 1, local * per, width), BF),
            pltpu.SemaphoreType.DMA((count,)),
            pltpu.SemaphoreType.DMA((parts,)),
            pltpu.SemaphoreType.DMA((local, 3)),
            pltpu.SemaphoreType.DMA((local,)),
        ],
        compiler_params=pltpu.CompilerParams(vmem_limit_bytes=VMEM_LIMIT),
        cost_estimate=pl.CostEstimate(
            flops=6 * local * slots_all * width * hidden,
            transcendentals=local * slots_all * hidden,
            bytes_accessed=6 * local * width * hidden + 4 * local * slots_all * width,
        ),
    )(slots, shares, *picked, *blocks, gate, up, down)
    return out[0], [out[1 + 3 * i : 4 + 3 * i] for i in range(count // 4)]


def spread(outs, total, half):
    for i in range(len(outs) // 3):
        base = 4 * half * i
        outs[3 * i][...] = total[base : base + half]
        outs[3 * i + 1][...] = total[base + half : base + 2 * half]
        outs[3 * i + 2][...] = total[base + 2 * half : base + 4 * half]


def combine(slots, y, groups, span, per, half):
    local = slots.shape[0]
    depth, width = y.shape[1:]
    each = span // (4 * half)
    outs_n = 3 * each * len(groups)

    def kernel(slots_ref, y_hbm, *refs):
        outs, y_ref, sem = refs[:outs_n], refs[outs_n], refs[outs_n + 1]
        copies = [
            pltpu.make_async_copy(y_hbm.at[g], y_ref.at[k], sem.at[k])
            for k, g in enumerate(groups)
        ]
        for copy in copies:
            copy.start()
        for k, g in enumerate(groups):
            chosen = chosen_rows(slots_ref, g, span, per, local)
            copies[k].wait()
            total = lax.dot_general(
                chosen, y_ref[k], (((0,), (0,)), ((), ())), preferred_element_type=F32
            ).astype(BF)
            spread(outs[3 * each * k : 3 * each * (k + 1)], total, half)

    vm = pl.BlockSpec(memory_space=pltpu.VMEM)
    out = pl.pallas_call(
        kernel,
        name="combine",
        out_shape=[
            jax.ShapeDtypeStruct(s, BF)
            for s in [(half, width), (half, width), (2 * half, width)] * (each * len(groups))
        ],
        in_specs=[vm, ANY],
        out_specs=[vm] * outs_n,
        scratch_shapes=[
            pltpu.VMEM((len(groups), depth, width), BF),
            pltpu.SemaphoreType.DMA((len(groups),)),
        ],
        compiler_params=pltpu.CompilerParams(vmem_limit_bytes=VMEM_LIMIT),
        cost_estimate=pl.CostEstimate(
            flops=2 * len(groups) * depth * span * width,
            transcendentals=0,
            bytes_accessed=2 * width * len(groups) * (span + depth),
        ),
    )(slots, y)
    return [out[3 * i : 3 * i + 3] for i in range(each * len(groups))]


def solution(mesh):
    groups = mesh.shape["groups"]
    devices = mesh.shape["tok"]
    cores = 2
    chips = devices // cores
    layer = max(1, 4 // groups)
    if chips % layer:
        layer = 1
    levels = chips // layer
    if layer == 2:
        order = [z * 2 for z in range(levels)] + [z * 2 + 1 for z in reversed(range(levels))]
    else:
        order = list(range(chips))
    position = [order.index(chip) for chip in range(chips)]
    reach = chips // 2

    def shift(step):
        pairs = []
        for at, chip in enumerate(order):
            for core in range(cores):
                pairs.append((chip * cores + core, order[(at + step) % chips] * cores + core))
        return pairs

    forward, backward = shift(1), shift(-1)
    swap = [(i, i ^ 1) for i in range(devices)]
    across = [(g, g ^ 1) for g in range(groups)]
    diagonal = [
        (g * devices + t, (g ^ 1) * devices + (t ^ 1))
        for g in range(groups)
        for t in range(devices)
    ]

    def to_forward(v):
        return lax.ppermute(v, "tok", forward)

    def to_backward(v):
        return lax.ppermute(v, "tok", backward)

    def to_sibling(v):
        return lax.ppermute(v, "tok", swap)

    def to_across(v):
        return lax.ppermute(v, "groups", across)

    def to_diagonal(v):
        return lax.ppermute(v, ("groups", "tok"), diagonal)

    def ring_gather(one, two):
        found = {0: [one, two]}
        ahead, back = [one, two], [one, two]
        for step in range(1, reach):
            for k in range(2):
                ahead[k] = to_forward(ahead[k])
                back[k] = to_backward(back[k])
            found[chips - step] = list(ahead)
            found[step] = list(back)
        found[reach] = [to_forward(ahead[0]), to_backward(back[1])]
        return found

    def add(*values):
        total = values[0].astype(F32)
        for value in values[1:]:
            total = total + value.astype(F32)
        return total.astype(BF)

    def after(value, *others):
        return lax.optimization_barrier((value,) + others)[0]

    def body(
        queries,
        new_keys,
        new_values,
        cache_keys,
        cache_values,
        cache_lens,
        residual,
        out_weight,
        norm_gain,
        expert_ids,
        route_weights,
        gate_weight,
        up_weight,
        down_weight,
    ):
        rows, width = residual.shape
        half = rows // 2
        local = gate_weight.shape[0]
        top = expert_ids.shape[1]
        capacity = max(2, BLOCK * top * 3 // (2 * local * devices))
        depth = out_weight.shape[0]
        cols = width // 4
        me = lax.axis_index("tok")
        core = me % cores
        quarter = (lax.axis_index("groups") % 2) * 2 + core
        mine = jnp.asarray(position, jnp.int32)[me // cores]
        near = [0] + [v for s in range(1, reach) for v in (s, chips - s)] + [reach]
        chip_at = jnp.asarray(order, jnp.int32)[(mine + jnp.asarray(near, jnp.int32)) % chips]

        own = lax.dynamic_slice_in_dim(out_weight, quarter * cols, cols, 1)
        other = to_sibling(lax.dynamic_slice_in_dim(out_weight, (quarter ^ 1) * cols, cols, 1))
        weights = ring_gather(own, other)

        meta = jnp.concatenate([expert_ids.T.astype(F32), route_weights.T], 0)[None]
        step = 1
        while step < devices:
            pairs = [(i, i ^ step) for i in range(devices)]
            meta = jnp.concatenate([meta, lax.ppermute(meta, "tok", pairs)], 0)
            step *= 2
        per_group = 2 * rows // BLOCK
        while per_group * capacity % 16 or per_group * BLOCK < 256:
            per_group *= 2
        span, per = per_group * BLOCK, per_group * capacity
        who = jnp.stack([chip_at * cores + core, chip_at * cores + (1 - core)], 1).reshape(-1)
        slots, shares = slot_tables(
            (who ^ me).astype(jnp.int32),
            (me * local).reshape(1).astype(jnp.int32),
            meta,
            local,
            top,
            capacity,
            per_group,
        )

        waits = [[]] + [
            [weights[s][k], weights[chips - s][k]] for s in range(1, reach) for k in range(2)
        ]
        pieces = [[], [], [], []]
        lens = cache_lens
        for kv in range(KVH):
            if kv < len(waits) and waits[kv]:
                lens = after(lens, *waits[kv])
            piece = attention_piece(
                lens, queries, new_keys, new_values, cache_keys, cache_values, kv
            )
            far = to_across(piece)
            pieces[0].append(piece)
            pieces[1].append(to_sibling(piece))
            pieces[2].append(far)
            pieces[3].append(to_sibling(far))

        first = chip_at * (cores * depth)
        table = jnp.stack([first + core * depth, first + (1 - core) * depth], 1).reshape(-1)
        table = after(table.astype(jnp.int32), slots)
        products = project(table, pieces, [w for o in near for w in weights[o]])
        columns = (quarter ^ jnp.arange(4)).astype(jnp.int32) * cols
        mixed, normed = [], []
        for k in range(2):
            returned = [
                products[0][k],
                to_sibling(products[1][k]),
                to_across(products[2][k]),
                to_diagonal(products[3][k]),
            ]
            m, n = mix_norm(columns, residual, norm_gain, returned, k)
            mixed.append(m)
            normed.append(n)

        found = ring_gather(*normed)
        for o in near:
            found[o] = found[o] + [to_sibling(v) for v in found[o]]
        each = span // (2 * rows)
        total = chips // each
        blocks = [
            [v for o in near[g * each : (g + 1) * each] for v in found[o]] for g in range(total)
        ]
        cuts = sorted(set([0, max(0, total - 3), total - 1]))
        picked = [
            select_rows(
                slots, [b for g in range(lo, hi) for b in blocks[g]], list(range(lo, hi)), span, per
            )
            for lo, hi in zip(cuts[:-1], cuts[1:])
        ]
        y, tail = experts(
            slots, shares, picked, blocks[-1], gate_weight, up_weight, down_weight, span, per
        )
        sums = {}
        for o, v in zip(near[(total - 1) * each :], tail):
            sums[o] = v
        for lo, hi in reversed(list(zip(cuts[:-1], cuts[1:]))):
            some = combine(slots, y, list(range(lo, hi)), span, per, half)
            for o, v in zip(near[lo * each : hi * each], some):
                sums[o] = v

        for o in reversed(near):
            one, two, theirs = sums[o]
            theirs = to_sibling(theirs)
            sums[o] = [[one, theirs[:half]], [two, theirs[half:]]]
        ahead, back = [None, None], [None, None]
        ahead[0] = to_forward(add(*sums[reach][0]))
        back[1] = to_backward(add(*sums[reach][1]))
        for step in range(reach - 1, 0, -1):
            for k in range(2):
                a = [] if ahead[k] is None else [ahead[k]]
                b = [] if back[k] is None else [back[k]]
                ahead[k] = to_forward(add(*sums[step][k], *a))
                back[k] = to_backward(add(*sums[chips - step][k], *b))
        final = []
        for k in range(2):
            value = mixed[k]
            for v in (*sums[0][k], ahead[k], back[k]):
                value = value + v.astype(F32)
            final.append(value.astype(BF))
        return jnp.concatenate(final, 0)

    placed = (
        P(("groups", "tok"), None),
        P(("groups", "tok"), None),
        P(("groups", "tok"), None),
        P(("groups", "tok"), None),
        P(("groups", "tok"), None),
        P(("groups", "tok")),
        P(("groups", "tok"), None),
        P("tok", None),
        P(),
        P(("groups", "tok"), None),
        P(("groups", "tok"), None),
        P("tok", None, None),
        P("tok", None, None),
        P("tok", None, None),
    )
    return jax.shard_map(
        body, mesh=mesh, in_specs=placed, out_specs=P(("groups", "tok"), None), check_vma=False
    )
```
